32 devices in a mesh: gx: 4 (over y, x), gy: 2 (over core), gz: 4 (over z).
Axes of the slice: x: 2, y: 2, z: 4, core: 2. Of those that a mesh axis runs over, the one named last changes fastest.
Arguments:
- positions: float32 [3, 4, 8, 16, 64], P(None, 'gz', 'gx', 'gy'), may hold values from 0 to 1
- counts: int32 [4, 8, 16], P('gz', 'gx', 'gy'), may hold values from 16 to 64, as said below
Outputs:
- force: float32 [3, 4, 8, 16, 64], P(None, 'gz', 'gx', 'gy')
- energy: float32 [4, 8, 16, 64], P('gz', 'gx', 'gy')
The draws below stay inside these ranges and needn't reach their ends.
Inputs may be any that keep to these rules, and one draw needn't show every extreme that they name: `counts`: every draw has some full cells.
All inputs are finite; a program needn't handle non-finite values.
Results may differ from the reference program's by a relative error of at most 0.0003.
Values sent between devices are 32-bit elements; how exact they have to be, the bound alone decides.
A program may use at most 64 MiB of HBM per device.

```python
import jax
import jax.numpy as jnp
from jax import lax

SLOTS = 64
NX = 8
NY = 16
NZ = 4


def draw_counts(key, part):
    first = jax.random.fold_in(key, 11)
    second = jax.random.fold_in(key, 23)
    base = jax.random.randint(first, (NZ, NX, NY), SLOTS // 4, 3 * SLOTS // 4 + 1)
    full = jax.random.randint(second, (NZ, NX, NY), 0, 16) == 0
    counts = jnp.where(full, SLOTS, base)
    counts = counts.at[0, 0, 0].set(SLOTS)
    return counts.astype(jnp.int32)


def block_levels(rng, extent, shards, least, largest):
    loudness, own = 1.0, jax.random.fold_in(rng, 6)
    for position, blocks in shards:
        draws = jnp.exp(jax.random.uniform(jax.random.fold_in(own, position), (blocks,), jnp.float32, least / len(shards), largest / len(shards)))
        loudness = loudness * jnp.repeat(draws, extent[position] // blocks).reshape([-1 if axis == position else 1 for axis in range(len(extent))])
    return loudness


def setup_inputs(seed: int = 0) -> dict:
    keys = jax.random.split(jax.random.key(seed), 3)
    return {
        "positions": jnp.clip(1.0 * jax.random.uniform(keys[0], (3, NZ, NX, NY, SLOTS), jnp.float32) ** block_levels(keys[0], (3, NZ, NX, NY, SLOTS), ((1, 4), (2, 4), (3, 2)), -0.2, 0.2), 0.0, 1.0),
        "counts": draw_counts(jax.random.fold_in(keys[2], 71), 0),
    }


cutoff_sq = 4.95 * 4.95
cell_sides = (12.0, 12.0, 2.5)
density_width = 8.0
pair_width = 3.0
density_amp = 1.0
pair_amp = 2.0

def kernels(squared):
    inside = jnp.where(squared < cutoff_sq, 1.0 - squared / cutoff_sq, 0.0)
    smooth = inside * inside
    smooth_slope = -2.0 * inside / cutoff_sq
    first = jnp.exp(-squared / density_width)
    second = jnp.exp(-squared / pair_width)
    return (density_amp * first * smooth, density_amp * first * (smooth_slope - smooth / density_width), pair_amp * second * smooth, pair_amp * second * (smooth_slope - smooth / pair_width))

def neighbours(extended, centre_z, start_x, start_y, rows_x, rows_y, step_z, step_x):
    pieces = []
    for step_y in (-1, 0, 1):
        pieces.append(extended[:, centre_z + step_z, start_x + step_x:start_x + step_x + rows_x, start_y + step_y:start_y + step_y + rows_y])
    return jnp.concatenate(pieces, axis=-1)

def pair_geometry(center, partner, step_z, step_x, slots):
    lateral = (jnp.arange(3 * slots) // slots - 1).astype(jnp.float32)
    moves = (float(step_x), lateral, float(step_z))
    squared = jnp.zeros((), jnp.float32)
    deltas = []
    for component in range(3):
        delta = (center[component][..., :, None] - partner[component][..., None, :] - moves[component]) * cell_sides[component]
        deltas.append(delta)
        squared = squared + delta * delta
    weight = center[3][..., :, None] * partner[3][..., None, :]
    if step_z == 0 and step_x == 0:
        column = jnp.arange(3 * slots)[None, :]
        row_index = jnp.arange(slots)[:, None]
        weight = weight * (column != row_index + slots).astype(jnp.float32)
    return (deltas, squared, weight)

def densities(extended, centre_z, start_x, start_y, rows_x, rows_y, slots):
    center = extended[:, centre_z, start_x:start_x + rows_x, start_y:start_y + rows_y]
    summed = jnp.zeros(center.shape[1:], jnp.float32)
    for step_z in range(-2, 3):
        for step_x in range(-1, 2):
            partner = neighbours(extended, centre_z, start_x, start_y, rows_x, rows_y, step_z, step_x)
            deltas, squared, weight = pair_geometry(center, partner, step_z, step_x, slots)
            summed = summed + lax.optimization_barrier(jnp.sum(weight * kernels(squared)[0], axis=-1))
    return summed

def forces(extended, centre_z, rows_x, rows_y, slots):
    center = extended[:, centre_z, 1:1 + rows_x, 1:1 + rows_y]
    pushes = [jnp.zeros(center.shape[1:], jnp.float32) for component in range(3)]
    pairs = jnp.zeros(center.shape[1:], jnp.float32)
    for step_z in range(-2, 3):
        for step_x in range(-1, 2):
            partner = neighbours(extended, centre_z, 1, 1, rows_x, rows_y, step_z, step_x)
            deltas, squared, weight = pair_geometry(center, partner, step_z, step_x, slots)
            values = kernels(squared)
            factor = weight * ((center[4][..., :, None] + partner[4][..., None, :]) * values[1] + values[3])
            pushes = [pushes[component] - 2.0 * lax.optimization_barrier(jnp.sum(factor * deltas[component], axis=-1)) for component in range(3)]
            pairs = pairs + lax.optimization_barrier(jnp.sum(weight * values[2], axis=-1))
    return (jnp.stack(pushes), pairs)

def reference(positions, counts):
    occupied = (jnp.arange(SLOTS)[None, None, None, :] < counts[..., None]).astype(jnp.float32)
    stacked = jnp.concatenate([positions, occupied[None]], axis=0)

    def window(source, layer):
        layers = ((layer + jnp.arange(-2, 3)) % NZ).astype(jnp.int32)
        taken = jnp.take(source, layers, axis=1)
        return jnp.pad(taken, ((0, 0), (0, 0), (1, 1), (1, 1), (0, 0)), mode='wrap')

    def first_pass(layer):
        return densities(window(stacked, layer), 2, 1, 1, NX, NY, SLOTS)
    density = lax.map(first_pass, jnp.arange(NZ))
    root = jnp.sqrt(1.0 + density)
    slope = -0.5 / root
    full = jnp.concatenate([stacked, slope[None]], axis=0)

    def second_pass(layer):
        return forces(window(full, layer), 2, NX, NY, SLOTS)
    pushes, pairs = lax.map(second_pass, jnp.arange(NZ))
    force = jnp.moveaxis(pushes, 0, 1)
    energy = occupied * (-root + 0.5 * pairs)
    return (force, energy)
```

```python
import functools
import math

import jax
import jax.numpy as jnp
from jax import lax
from jax.experimental import pallas as pl
from jax.experimental.pallas import tpu as pltpu
from jax.sharding import PartitionSpec as P

CUT = 4.95
SIDES = (12.0, 12.0, 2.5)
FAR = 1024.0
LOG2E = math.log2(math.e)
SCALE = math.sqrt(LOG2E / 8.0)
REACH = CUT * CUT * LOG2E / 8.0
EDGE = (CUT + 0.01) / SIDES[0]
A = 2.0 * LOG2E
B = 0.75 * LOG2E
G1 = 2.0 ** (-REACH) / REACH**2
G2 = 2.0 ** (-REACH * 8.0 / 3.0) / REACH**2
DEPTH = 2
LAYERS = 2 * DEPTH + 1
VMEM = pl.BlockSpec(memory_space=pltpu.VMEM)
SMEM = pl.BlockSpec(memory_space=pltpu.SMEM)


def shifted(x, axis, distance):
    n = lax.axis_size(axis)
    return lax.ppermute(x, axis, [(i, (i + distance) % n) for i in range(n)])


def exchange(x):
    x = jnp.concatenate([shifted(x[-1:], "gx", 1), x, shifted(x[:1], "gx", -1)], axis=0)
    x = jnp.concatenate(
        [shifted(x[:, -1:], "gy", 1), x, shifted(x[:, :1], "gy", -1)], axis=1
    )
    nz = lax.axis_size("gz")
    got = {0: x}
    layers = []
    for a in range(-DEPTH, DEPTH + 1):
        if a % nz not in got:
            got[a % nz] = shifted(x, "gz", -a)
        layers.append(got[a % nz])
    return jnp.stack(layers)


def iota(shape, dim):
    return lax.broadcasted_iota(jnp.int32, shape, dim)


def coordinates(row, c, z, x, tile, half):
    width = row.shape[-1]
    if c == 2:
        cell = z
    elif c == 0:
        cell = x
    else:
        cell = 2 * tile + (iota((1, width), 1) >= half).astype(jnp.int32)
    cell = jnp.asarray(cell, jnp.int32)
    return (row + cell.astype(jnp.float32)) * (SIDES[c] * SCALE)


def prep_kernel(rx, nt, half, own_ref, cen_ref, slot_ref):
    width = 2 * half
    sub = iota((width, width), 0)
    lane = iota((width, width), 1)
    eye = sub == lane
    same = sub // half == lane // half
    before = sub < lane
    base = jnp.where(iota((1, width), 1) >= half, half, 0)

    def step(i, carry):
        x, t = i // nt, i % nt
        rows = [own_ref[x, t, c : c + 1, :] for c in range(3)]
        key = jnp.broadcast_to(rows[0], (width, width))
        column = jnp.sum(jnp.where(eye, key, 0.0), axis=1, keepdims=True)
        ahead = same & ((column < key) | ((column == key) & before))
        rank = jnp.sum(ahead.astype(jnp.float32), axis=0, keepdims=True)
        slot = rank.astype(jnp.int32) + base
        slot_ref[x, t] = slot
        pick = sub == slot
        for c in range(3):
            row = coordinates(rows[c], c, 0, x, t, half)
            column = jnp.sum(jnp.where(pick, row, 0.0), axis=1, keepdims=True)
            cen_ref[x, t, c] = jnp.broadcast_to(column, (width, width))
        return carry

    lax.fori_loop(0, rx * nt, step, 0)


def replicate(rx, nt, half, ext_ref, rep_ref, channels, first, absolute):
    width = 2 * half
    low = iota((1, width), 1) < half

    def step(i, carry):
        x, t = i // nt, i % nt
        for z in range(LAYERS):
            for c in range(channels):
                rows = []
                for u in (0, 1, 2):
                    row = ext_ref[z, x, t + u, c : c + 1, :]
                    if absolute:
                        row = coordinates(row, c, z - DEPTH, x - 1, t + u - 1, half)
                    rows.append(row)
                mixed = jnp.where(low, rows[2], rows[0])
                rep_ref[x, t, z, first + c] = jnp.broadcast_to(rows[1], (8, width))
                rep_ref[x, t, z, channels_total(rep_ref) // 2 + first + c] = (
                    jnp.broadcast_to(mixed, (8, width))
                )
        return carry

    lax.fori_loop(0, (rx + 2) * nt, step, 0)


def channels_total(rep_ref):
    return rep_ref.shape[3]


def separation(centre, partner):
    deltas = [p - q for p, q in zip(centre, partner)]
    t = REACH - deltas[0] * deltas[0]
    t = t - deltas[1] * deltas[1]
    t = t - deltas[2] * deltas[2]
    return deltas, jnp.maximum(t, 0.0)


def bounds(bound_ref, x, t, group):
    left = jnp.maximum(bound_ref[1, x, 2 * t], bound_ref[1, x, 2 * t + 1])
    start = group * 8
    first = jnp.where(start < left, 0, 1)
    right = (
        (start + 8 > bound_ref[2, x, 2 * t]) & (start < bound_ref[0, x, 2 * t])
    ) | (
        (start + 8 > bound_ref[2, x, 2 * t + 1]) & (start < bound_ref[0, x, 2 * t + 1])
    )
    return first, jnp.where(right, 3, 2)


def groups_of(bound_ref, x, t):
    most = jnp.maximum(bound_ref[0, x, 2 * t], bound_ref[0, x, 2 * t + 1])
    return (most + 7) // 8


def occupied_lanes(bound_ref, x, t, half):
    lane = iota((1, 2 * half), 1)
    n0, n1 = bound_ref[0, x, 2 * t], bound_ref[0, x, 2 * t + 1]
    return jnp.where(lane < half, lane - n0, lane - half - n1) < 0


def centres(ref, index, start, half, low):
    c0 = ref[index + (pl.ds(start, 8),)]
    c1 = ref[index + (pl.ds(half + start, 8),)]
    return c0, c1, jnp.where(low, c1, c0)


def totals(acc, low):
    zero = jnp.zeros_like(acc[2])
    s0 = jnp.sum(acc[0] + jnp.where(low, zero, acc[2]), axis=1, keepdims=True)
    s1 = jnp.sum(acc[1] + jnp.where(low, acc[2], zero), axis=1, keepdims=True)
    return s0, s1


def density_kernel(
    rx, nt, half, bound_ref, ext_ref, cen_ref, slot_ref, slope_ref, root_ref, cs_ref, rep
):
    width = 2 * half
    low = iota((8, width), 1) < half
    replicate(rx, nt, half, ext_ref, rep, 3, 0, True)
    sub = iota((width, width), 0)

    def tile(i, carry):
        x, t = i // nt, i % nt

        def group(g, carry):
            start = pl.multiple_of(g * 8, 8)
            cs = [centres(cen_ref, (x, t, c), start, half, low) for c in range(3)]
            first, last = bounds(bound_ref, x, t, g)

            def column(dx, acc):
                acc = list(acc)
                for z in range(LAYERS):
                    for k in range(3):
                        partner = [
                            rep[x + dx, t, z, (3 if k == 2 else 0) + c] for c in range(3)
                        ]
                        _, v = separation([c[k] for c in cs], partner)
                        acc[k] = acc[k] + jnp.exp2(v) * (v * v)
                return tuple(acc)

            zero = jnp.zeros((8, width), jnp.float32)
            acc = lax.fori_loop(first, last, column, (zero,) * 3)
            for k, total in enumerate(totals(acc, low)):
                cs_ref[x, t, pl.ds(k * half + start, 8)] = jnp.broadcast_to(
                    total * G1, (8, width)
                )
            return carry

        lax.fori_loop(0, groups_of(bound_ref, x, t), group, 0)
        pick = sub == slot_ref[x, t]
        one_rho = jnp.sum(jnp.where(pick, cs_ref[x, t], 0.0), axis=0, keepdims=True)
        occupied = occupied_lanes(bound_ref, x, t, half)
        root = jnp.sqrt(jnp.where(occupied, one_rho, 1.0))
        root_ref[x, t] = root
        slope_ref[x, t] = -0.5 / root
        cs_ref[x, t] = -0.5 * lax.rsqrt(cs_ref[x, t])
        return carry

    lax.fori_loop(0, rx * nt, tile, 0)


SIGMA = (3.0 / 16.0) * G1 / G2


def force_kernel(
    rx, nt, half, bound_ref, ext_ref, sext_ref, cen_ref, cs_ref, slot_ref, root_ref,
    force_ref, energy_ref, rep, out,
):
    width = 2 * half
    low = iota((8, width), 1) < half
    replicate(rx, nt, half, ext_ref, rep, 3, 0, True)
    replicate(rx, nt, half, sext_ref, rep, 1, 3, False)
    sub = iota((width, width), 0)

    def tile(i, carry):
        x, t = i // nt, i % nt

        def group(g, carry):
            start = pl.multiple_of(g * 8, 8)
            cs = [centres(cen_ref, (x, t, c), start, half, low) for c in range(3)]
            sp = [s * SIGMA for s in centres(cs_ref, (x, t), start, half, low)]
            first, last = bounds(bound_ref, x, t, g)

            def column(dx, acc):
                acc = [list(a) for a in acc]
                for z in range(LAYERS):
                    for k in range(3):
                        partner = [
                            rep[x + dx, t, z, (4 if k == 2 else 0) + c] for c in range(4)
                        ]
                        d, v = separation([c[k] for c in cs], partner[:3])
                        e1 = jnp.exp2(v)
                        e2 = jnp.exp2(v * (8.0 / 3.0))
                        w = v * e2
                        factor = (sp[k] + partner[3]) * e1 * (v + A) * v + w * (v + B)
                        for c in range(3):
                            acc[c][k] = acc[c][k] + factor * d[c]
                        acc[3][k] = acc[3][k] + w * v
                return tuple(tuple(a) for a in acc)

            zero = jnp.zeros((8, width), jnp.float32)
            acc = lax.fori_loop(first, last, column, ((zero,) * 3,) * 4)
            for c in range(4):
                for k, total in enumerate(totals(acc[c], low)):
                    out[c, pl.ds(k * half + start, 8)] = jnp.broadcast_to(total, (8, width))
            return carry

        lax.fori_loop(0, groups_of(bound_ref, x, t), group, 0)
        pick = sub == slot_ref[x, t]
        occupied = occupied_lanes(bound_ref, x, t, half)
        for c in range(4):
            value = jnp.sum(jnp.where(pick, out[c], 0.0), axis=0, keepdims=True)
            if c < 3:
                value = value * (4.0 / 3.0 * G2 / SCALE)
                force_ref[c, x, t] = jnp.where(occupied, value, 0.0)
            else:
                value = value * G2 - 1.0 - root_ref[x, t]
                energy_ref[x, t] = jnp.where(occupied, value, 0.0)
        return carry

    lax.fori_loop(0, rx * nt, tile, 0)


def body(positions, counts):
    rx, ry, half = positions.shape[2:]
    nt, width = ry // 2, 2 * half
    f32 = jnp.float32

    def shape(*dims, dtype=f32):
        return jax.ShapeDtypeStruct(dims, dtype)

    occupied = jnp.arange(half) < counts[0][..., None]
    u = jnp.where(occupied, positions[:, 0], FAR)
    left = jnp.sum(u[0] < EDGE, axis=-1, dtype=jnp.int32)
    right = jnp.sum(u[0] < 1.0 - EDGE, axis=-1, dtype=jnp.int32)
    bound = jnp.stack([counts[0], left, right])
    own = jnp.moveaxis(u.reshape(3, rx, nt, width), 0, 2)
    cen, slot = pl.pallas_call(
        functools.partial(prep_kernel, rx, nt, half),
        out_shape=(
            shape(rx, nt, 3, width, width),
            shape(rx, nt, 1, width, dtype=jnp.int32),
        ),
        in_specs=[VMEM],
        out_specs=(VMEM, VMEM),
        cost_estimate=pl.CostEstimate(
            flops=20 * rx * nt * width * width, bytes_accessed=12 * rx * nt * width * width, transcendentals=0
        ),
        name="prep",
    )(own)
    ext = exchange(own)
    slope, root, cs = pl.pallas_call(
        functools.partial(density_kernel, rx, nt, half),
        out_shape=(
            shape(rx, nt, 1, width),
            shape(rx, nt, 1, width),
            shape(rx, nt, width, width),
        ),
        in_specs=[SMEM, VMEM, VMEM, VMEM],
        out_specs=(VMEM, VMEM, VMEM),
        scratch_shapes=[pltpu.VMEM((rx + 2, nt, LAYERS, 6, 8, width), f32)],
        name="density",
    )(bound, ext, cen, slot)
    sext = exchange(slope * SIGMA)
    force, energy = pl.pallas_call(
        functools.partial(force_kernel, rx, nt, half),
        out_shape=(shape(3, rx, nt, 1, width), shape(rx, nt, 1, width)),
        in_specs=[SMEM] + [VMEM] * 6,
        out_specs=(VMEM, VMEM),
        scratch_shapes=[
            pltpu.VMEM((rx + 2, nt, LAYERS, 8, 8, width), f32),
            pltpu.VMEM((4, width, width), f32),
        ],
        name="force",
    )(bound, ext, sext, cen, cs, slot, root)
    return force.reshape(3, 1, rx, ry, half), energy.reshape(1, rx, ry, half)


def solution(mesh):
    return jax.shard_map(
        body,
        mesh=mesh,
        in_specs=(P(None, "gz", "gx", "gy", None), P("gz", "gx", "gy")),
        out_specs=(P(None, "gz", "gx", "gy", None), P("gz", "gx", "gy", None)),
        check_vma=False,
    )
```

```python
import functools
import math

import jax
import jax.numpy as jnp
from jax import lax
from jax.experimental import pallas as pl
from jax.experimental.pallas import tpu as pltpu
from jax.sharding import PartitionSpec as P

CUT = 4.95
SIDES = (12.0, 12.0, 2.5)
FAR = 1024.0
LOG2E = math.log2(math.e)
SCALE = math.sqrt(LOG2E / 8.0)
REACH = CUT * CUT * LOG2E / 8.0
EDGE = (CUT + 0.01) / SIDES[0]
A = 2.0 * LOG2E
B = 0.75 * LOG2E
G1 = 2.0 ** (-REACH) / REACH**2
G2 = 2.0 ** (-REACH * 8.0 / 3.0) / REACH**2
DEPTH = 2
LAYERS = 2 * DEPTH + 1
VMEM = pl.BlockSpec(memory_space=pltpu.VMEM)
SMEM = pl.BlockSpec(memory_space=pltpu.SMEM)


AXES = ("gz", "gx", "gy")


def layer_slots(nz):
    kept = []
    for a in range(-DEPTH, DEPTH + 1):
        if all((a - k) % nz for k in kept):
            kept.append(a)
    slot = [
        next(i for i, k in enumerate(kept) if (a - k) % nz == 0)
        for a in range(-DEPTH, DEPTH + 1)
    ]
    return kept, slot


def displacements(sizes):
    kept, _ = layer_slots(sizes[0])
    copies, others = [], []
    for s, a in enumerate(kept):
        for b in (-1, 0, 1):
            for c in (-1, 0, 1):
                if (a, b, c) == (0, 0, 0):
                    continue
                step = tuple(-o % n for o, n in zip((a, b, c), sizes))
                copies.append((s, b, c, step))
                if any(step) and step not in others:
                    others.append(step)
    return copies, others


def device(step, sizes):
    return {
        axis: lax.rem(lax.axis_index(axis) + d, n)
        for axis, d, n in zip(AXES, step, sizes)
    }


def enter(sizes):
    _, others = displacements(sizes)
    barrier = pltpu.get_barrier_semaphore()
    for step in others:
        pl.semaphore_signal(
            barrier,
            inc=1,
            device_id=device(step, sizes),
            device_id_type=pl.DeviceIdType.MESH,
        )
    return barrier, len(others)


def edge(offset, length):
    if offset == 0:
        return pl.ds(0, length), pl.ds(1, length)
    if offset < 0:
        return pl.ds(length - 1, 1), pl.ds(0, 1)
    return pl.ds(0, 1), pl.ds(length + 1, 1)


def start_copies(sizes, rx, nt, own, ext, send, recv):
    copies, _ = displacements(sizes)
    started = []
    for i, (s, b, c, step) in enumerate(copies):
        (sx, dx), (st, dt) = edge(b, rx), edge(c, nt)
        source, target = own.at[sx, st], ext.at[s, dx, dt]
        if any(step):
            copy = pltpu.make_async_remote_copy(
                src_ref=source,
                dst_ref=target,
                send_sem=send.at[i],
                recv_sem=recv.at[i],
                device_id=device(step, sizes),
                device_id_type=pl.DeviceIdType.MESH,
            )
        else:
            copy = pltpu.make_async_copy(source, target, recv.at[i])
        copy.start()
        started.append(copy)
    return started


def iota(shape, dim):
    return lax.broadcasted_iota(jnp.int32, shape, dim)


def coordinates(row, c, z, x, tile, half):
    width = row.shape[-1]
    if c == 2:
        cell = z
    elif c == 0:
        cell = x
    else:
        cell = 2 * tile + (iota((1, width), 1) >= half).astype(jnp.int32)
    cell = jnp.asarray(cell, jnp.int32)
    return (row + cell.astype(jnp.float32)) * (SIDES[c] * SCALE)


def halo_kernel(
    sizes, rx, nt, half, count_ref, pos_ref, ext_ref, cen_ref, slot_ref, bound_ref, own, send, recv
):
    barrier, arrivals = enter(sizes)
    width = 2 * half
    home = layer_slots(sizes[0])[1][DEPTH]
    wide = iota((1, width), 1)
    for x in range(rx):
        for t in range(nt):
            occupied = occupied_lanes(count_ref, x, t, half)
            for c in range(3):
                rows = [pos_ref[c, 0, x, 2 * t + k : 2 * t + k + 1, :] for k in (0, 1)]
                row = jnp.where(occupied, jnp.concatenate(rows, axis=1), FAR)
                own[x, t, c] = row
                ext_ref[home, x + 1, t + 1, c] = row
    pl.semaphore_wait(barrier, arrivals)
    copies = start_copies(sizes, rx, nt, own, ext_ref, send, recv)

    sub = iota((width, width), 0)
    lane = iota((width, width), 1)
    eye = sub == lane
    same = sub // half == lane // half
    before = sub < lane
    base = jnp.where(wide >= half, half, 0)
    weight = jnp.where(wide >= half, 256.0, 1.0)

    def step(i, carry):
        x, t = i // nt, i % nt
        rows = [own[x, t, c] for c in range(3)]
        bound_ref[0, x, t] = jnp.sum(jnp.where(rows[0] < EDGE, weight, 0.0)).astype(jnp.int32)
        bound_ref[1, x, t] = jnp.sum(jnp.where(rows[0] < 1.0 - EDGE, weight, 0.0)).astype(
            jnp.int32
        )
        key = jnp.broadcast_to(rows[0], (width, width))
        column = jnp.sum(jnp.where(eye, key, 0.0), axis=1, keepdims=True)
        ahead = same & ((column < key) | ((column == key) & before))
        rank = jnp.sum(ahead.astype(jnp.float32), axis=0, keepdims=True)
        slot = rank.astype(jnp.int32) + base
        slot_ref[x, t] = slot
        pick = sub == slot
        for c in range(3):
            row = coordinates(rows[c], c, 0, x, t, half)
            column = jnp.sum(jnp.where(pick, row, 0.0), axis=1, keepdims=True)
            cen_ref[x, t, c] = jnp.broadcast_to(column, (width, width))
        return carry

    lax.fori_loop(0, rx * nt, step, 0, unroll=2)
    for copy in copies:
        copy.wait()


def slope_kernel(sizes, rx, nt, own_ref, ext_ref, send, recv):
    barrier, arrivals = enter(sizes)
    home = layer_slots(sizes[0])[1][DEPTH]
    for x in range(rx):
        for t in range(nt):
            ext_ref[home, x + 1, t + 1, 0] = own_ref[x, t, 0]
    pl.semaphore_wait(barrier, arrivals)
    for copy in start_copies(sizes, rx, nt, own_ref, ext_ref, send, recv):
        copy.wait()


def replicate(slots, rx, nt, half, ext_ref, rep_ref, channels, first, absolute):
    width = 2 * half
    low = iota((1, width), 1) < half

    def step(i, carry):
        x, t = i // nt, i % nt
        for z in range(LAYERS):
            for c in range(channels):
                rows = []
                for u in (0, 1, 2):
                    row = ext_ref[slots[z], x, t + u, c]
                    if absolute:
                        row = coordinates(row, c, z - DEPTH, x - 1, t + u - 1, half)
                    rows.append(row)
                mixed = jnp.where(low, rows[2], rows[0])
                rep_ref[x, t, z, first + c] = jnp.broadcast_to(rows[1], (8, width))
                rep_ref[x, t, z, channels_total(rep_ref) // 2 + first + c] = (
                    jnp.broadcast_to(mixed, (8, width))
                )
        return carry

    lax.fori_loop(0, (rx + 2) * nt, step, 0)


def channels_total(rep_ref):
    return rep_ref.shape[3]


def separation(centre, partner):
    deltas = [p - q for p, q in zip(centre, partner)]
    t = REACH - deltas[0] * deltas[0]
    t = t - deltas[1] * deltas[1]
    t = t - deltas[2] * deltas[2]
    return deltas, jnp.maximum(t, 0.0)


def bounds(count_ref, bound_ref, x, t, start, rows):
    lefts, rights = bound_ref[0, x, t], bound_ref[1, x, t]
    left = jnp.maximum(lefts & 255, lefts >> 8)
    first = jnp.where(start < left, 0, 1)
    right = False
    for k, inner in enumerate((rights & 255, rights >> 8)):
        right |= (start + rows > inner) & (start < count_ref[0, x, 2 * t + k])
    return first, jnp.where(right & (first == 0), 3, first + 2)


def groups_of(count_ref, x, t, rows):
    most = jnp.maximum(count_ref[0, x, 2 * t], count_ref[0, x, 2 * t + 1])
    return (most + (rows - 1)) // rows


def occupied_lanes(count_ref, x, t, half):
    lane = iota((1, 2 * half), 1)
    n0, n1 = count_ref[0, x, 2 * t], count_ref[0, x, 2 * t + 1]
    return jnp.where(lane < half, lane - n0, lane - half - n1) < 0


def centres(ref, index, start, rows, half):
    low = iota((rows, 2 * half), 1) < half
    c0 = ref[index + (pl.ds(start, rows),)]
    c1 = ref[index + (pl.ds(half + start, rows),)]
    return c0, c1, jnp.where(low, c1, c0)


def combined(acc, half):
    low = iota(acc[2].shape, 1) < half
    zero = jnp.zeros_like(acc[2])
    return (
        acc[0] + jnp.where(low, zero, acc[2]),
        acc[1] + jnp.where(low, acc[2], zero),
    )


def over(partner, rows):
    return partner if rows == 8 else jnp.concatenate([partner] * (rows // 8), axis=0)


def columns(one, first, last, acc):
    acc = one(first + 1, one(first, acc))
    return lax.fori_loop(first + 2, last, one, acc)


def density_kernel(
    slots, rx, nt, half, rows, count_ref, bound_ref, ext_ref, cen_ref, slot_ref,
    slope_ref, root_ref, cs_ref, rep,
):
    width = 2 * half
    replicate(slots, rx, nt, half, ext_ref, rep, 3, 0, True)
    sub = iota((width, width), 0)

    def tile(i, carry):
        x, t = i // nt, i % nt

        def group(g, carry):
            start = pl.multiple_of(g * rows, rows)
            cs = [centres(cen_ref, (x, t, c), start, rows, half) for c in range(3)]
            first, last = bounds(count_ref, bound_ref, x, t, start, rows)

            def column(dx, acc):
                acc = list(acc)
                for z in range(LAYERS):
                    for k in range(3):
                        partner = [
                            over(rep[x + dx, t, z, (3 if k == 2 else 0) + c], rows)
                            for c in range(3)
                        ]
                        _, v = separation([c[k] for c in cs], partner)
                        acc[k] = acc[k] + jnp.exp2(v) * (v * v)
                return tuple(acc)

            zero = jnp.zeros((rows, width), jnp.float32)
            acc = columns(column, first, last, (zero,) * 3)
            for k, part in enumerate(combined(acc, half)):
                cs_ref[x, t, pl.ds(k * half + start, rows)] = part
            return carry

        lax.fori_loop(0, groups_of(count_ref, x, t, rows), group, 0)
        total = jnp.sum(cs_ref[x, t], axis=1, keepdims=True) * G1
        pick = sub == slot_ref[x, t]
        one_rho = jnp.sum(jnp.where(pick, total, 0.0), axis=0, keepdims=True)
        occupied = occupied_lanes(count_ref, x, t, half)
        root = jnp.sqrt(jnp.where(occupied, one_rho, 1.0))
        root_ref[x, t] = root
        slope_ref[x, t, 0] = (-0.5 * SIGMA) / root
        cs_ref[x, t] = jnp.broadcast_to((-0.5 * SIGMA) * lax.rsqrt(total), (width, width))
        return carry

    lax.fori_loop(0, rx * nt, tile, 0)


SIGMA = (3.0 / 16.0) * G1 / G2


def force_kernel(
    slots, rx, nt, half, rows, count_ref, bound_ref, ext_ref, sext_ref, cen_ref, cs_ref,
    slot_ref, root_ref, force_ref, energy_ref, rep, out,
):
    width = 2 * half
    replicate(slots, rx, nt, half, ext_ref, rep, 3, 0, True)
    replicate(slots, rx, nt, half, sext_ref, rep, 1, 3, False)
    sub = iota((width, width), 0)

    for x in range(rx):
        for t in range(nt):
            force_tile(
                slots, half, rows, x, t, count_ref, bound_ref, cen_ref, cs_ref, slot_ref,
                root_ref, force_ref, energy_ref, rep, out, sub,
            )


def force_tile(
    slots, half, rows, x, t, count_ref, bound_ref, cen_ref, cs_ref, slot_ref, root_ref,
    force_ref, energy_ref, rep, out, sub,
):
    width = 2 * half

    def group(g, carry):
        start = pl.multiple_of(g * rows, rows)
        cs = [centres(cen_ref, (x, t, c), start, rows, half) for c in range(3)]
        sp = centres(cs_ref, (x, t), start, rows, half)
        first, last = bounds(count_ref, bound_ref, x, t, start, rows)

        def column(dx, acc):
            acc = [list(a) for a in acc]
            for z in range(LAYERS):
                for k in range(3):
                    partner = [
                        over(rep[x + dx, t, z, (4 if k == 2 else 0) + c], rows)
                        for c in range(4)
                    ]
                    d, v = separation([c[k] for c in cs], partner[:3])
                    e1 = jnp.exp2(v)
                    e2 = jnp.exp2(v * (8.0 / 3.0))
                    w = v * e2
                    factor = (sp[k] + partner[3]) * e1 * (v + A) * v + w * (v + B)
                    for c in range(3):
                        acc[c][k] = acc[c][k] + factor * d[c]
                    acc[3][k] = acc[3][k] + w * v
            return tuple(tuple(a) for a in acc)

        zero = jnp.zeros((rows, width), jnp.float32)
        acc = columns(column, first, last, ((zero,) * 3,) * 4)
        for c in range(4):
            for k, part in enumerate(combined(acc[c], half)):
                out[c, pl.ds(k * half + start, rows)] = part
        return carry

    lax.fori_loop(0, groups_of(count_ref, x, t, rows), group, 0)
    pick = sub == slot_ref[x, t]
    occupied = occupied_lanes(count_ref, x, t, half)
    for c in range(4):
        total = jnp.sum(out[c], axis=1, keepdims=True)
        value = jnp.sum(jnp.where(pick, total, 0.0), axis=0, keepdims=True)
        if c < 3:
            value = value * (4.0 / 3.0 * G2 / SCALE)
        else:
            value = value * G2 - 1.0 - root_ref[x, t]
        value = jnp.where(occupied, value, 0.0)
        for k in (0, 1):
            part = value[:, k * half : (k + 1) * half]
            if c < 3:
                force_ref[c, 0, x, 2 * t + k : 2 * t + k + 1, :] = part
            else:
                energy_ref[0, x, 2 * t + k : 2 * t + k + 1, :] = part


def body(positions, counts):
    rx, ry, half = positions.shape[2:]
    nt, width = ry // 2, 2 * half
    f32 = jnp.float32
    sizes = tuple(lax.axis_size(axis) for axis in AXES)
    kept, slots = layer_slots(sizes[0])
    links = len(displacements(sizes)[0])
    sems = [pltpu.SemaphoreType.DMA((links,))] * 2

    def shape(*dims, dtype=f32):
        return jax.ShapeDtypeStruct(dims, dtype)

    ext, cen, slot, bound = pl.pallas_call(
        functools.partial(halo_kernel, sizes, rx, nt, half),
        out_shape=(
            shape(len(kept), rx + 2, nt + 2, 3, 1, width),
            shape(rx, nt, 3, width, width),
            shape(rx, nt, 1, width, dtype=jnp.int32),
            shape(2, rx, nt, dtype=jnp.int32),
        ),
        in_specs=[SMEM, VMEM],
        out_specs=(VMEM, VMEM, VMEM, SMEM),
        scratch_shapes=[pltpu.VMEM((rx, nt, 3, 1, width), f32)] + sems,
        compiler_params=pltpu.CompilerParams(collective_id=0, has_side_effects=True),
        name="halo",
    )(counts, positions)
    slope, root, cs = pl.pallas_call(
        functools.partial(density_kernel, slots, rx, nt, half, 16),
        out_shape=(
            shape(rx, nt, 1, 1, width),
            shape(rx, nt, 1, width),
            shape(rx, nt, width, width),
        ),
        in_specs=[SMEM, SMEM] + [VMEM] * 3,
        out_specs=(VMEM, VMEM, VMEM),
        scratch_shapes=[pltpu.VMEM((rx + 2, nt, LAYERS, 6, 8, width), f32)],
        name="density",
    )(counts, bound, ext, cen, slot)
    sext = pl.pallas_call(
        functools.partial(slope_kernel, sizes, rx, nt),
        out_shape=shape(len(kept), rx + 2, nt + 2, 1, 1, width),
        in_specs=[VMEM],
        out_specs=VMEM,
        scratch_shapes=sems,
        compiler_params=pltpu.CompilerParams(collective_id=1, has_side_effects=True),
        name="slopes",
    )(slope)
    return pl.pallas_call(
        functools.partial(force_kernel, slots, rx, nt, half, 8),
        out_shape=(shape(3, 1, rx, ry, half), shape(1, rx, ry, half)),
        in_specs=[SMEM, SMEM] + [VMEM] * 6,
        out_specs=(VMEM, VMEM),
        scratch_shapes=[
            pltpu.VMEM((rx + 2, nt, LAYERS, 8, 8, width), f32),
            pltpu.VMEM((4, width, width), f32),
        ],
        name="force",
    )(counts, bound, ext, sext, cen, cs, slot, root)


def solution(mesh):
    return jax.shard_map(
        body,
        mesh=mesh,
        in_specs=(P(None, "gz", "gx", "gy", None), P("gz", "gx", "gy")),
        out_specs=(P(None, "gz", "gx", "gy", None), P("gz", "gx", "gy", None)),
        check_vma=False,
    )
```

```python
import functools
import math

import jax
import jax.numpy as jnp
from jax import lax
from jax.experimental import pallas as pl
from jax.experimental.pallas import tpu as pltpu
from jax.sharding import PartitionSpec as P

CUT = 4.95
SIDES = (12.0, 12.0, 2.5)
FAR = 1024.0
LOG2E = math.log2(math.e)
SCALE = math.sqrt(LOG2E / 8.0)
REACH = CUT * CUT * LOG2E / 8.0
EDGE = (CUT + 0.01) / SIDES[0]
A = 2.0 * LOG2E
B = 0.75 * LOG2E
G1 = 2.0 ** (-REACH) / REACH**2
G2 = 2.0 ** (-REACH * 8.0 / 3.0) / REACH**2
DEPTH = 2
LAYERS = 2 * DEPTH + 1
VMEM = pl.BlockSpec(memory_space=pltpu.VMEM)
ANY = pl.BlockSpec(memory_space=pl.ANY)
SMEM = pl.BlockSpec(memory_space=pltpu.SMEM)


AXES = ("gz", "gx", "gy")


def layer_slots(nz):
    kept = []
    for a in range(-DEPTH, DEPTH + 1):
        if all((a - k) % nz for k in kept):
            kept.append(a)
    slot = [
        next(i for i, k in enumerate(kept) if (a - k) % nz == 0)
        for a in range(-DEPTH, DEPTH + 1)
    ]
    return kept, slot


def displacements(sizes):
    kept, _ = layer_slots(sizes[0])
    layers = [(s, (-a % sizes[0], 0, 0)) for s, a in enumerate(kept) if a]
    edges = [
        (b, c, (0, -b % sizes[1], -c % sizes[2]))
        for b in (-1, 0, 1)
        for c in (-1, 0, 1)
        if b or c
    ]
    others = []
    for step in [layer[-1] for layer in layers] + [e[-1] for e in edges]:
        if any(step) and step not in others:
            others.append(step)
    return layers, edges, others


def device(step, sizes):
    return {
        axis: lax.rem(lax.axis_index(axis) + d, n)
        for axis, d, n in zip(AXES, step, sizes)
    }


def enter(sizes):
    others = displacements(sizes)[2]
    barrier = pltpu.get_barrier_semaphore()
    for step in others:
        pl.semaphore_signal(
            barrier,
            inc=1,
            device_id=device(step, sizes),
            device_id_type=pl.DeviceIdType.MESH,
        )
    return barrier, len(others)


def edge(offset, length):
    if offset == 0:
        return pl.ds(1, length), pl.ds(1, length)
    if offset < 0:
        return pl.ds(length, 1), pl.ds(0, 1)
    return pl.ds(1, 1), pl.ds(length + 1, 1)


def start(source, target, step, sizes, send, recv):
    if any(step):
        copy = pltpu.make_async_remote_copy(
            src_ref=source,
            dst_ref=target,
            send_sem=send,
            recv_sem=recv,
            device_id=device(step, sizes),
            device_id_type=pl.DeviceIdType.MESH,
        )
    else:
        copy = pltpu.make_async_copy(source, target, recv)
    copy.start()
    return copy


def exchange(sizes, rx, nt, own, ext, send, recv, beside=(None, None)):
    layers, edges, _ = displacements(sizes)
    copies = [
        start(
            own, ext.at[s, pl.ds(1, rx), pl.ds(1, nt)], step, sizes, send.at[i], recv.at[i]
        )
        for i, (s, step) in enumerate(layers)
    ]
    if beside[0]:
        beside[0]()
    for copy in copies:
        copy.wait()
    copies = []
    for i, (b, c, step) in enumerate(edges, len(layers)):
        (sx, dx), (st, dt) = edge(b, rx), edge(c, nt)
        copies.append(
            start(ext.at[:, sx, st], ext.at[:, dx, dt], step, sizes, send.at[i], recv.at[i])
        )
    if beside[1]:
        beside[1]()
    for copy in copies:
        copy.wait()


def iota(shape, dim):
    return lax.broadcasted_iota(jnp.int32, shape, dim)


def coordinates(row, c, z, x, tile, half):
    width = row.shape[-1]
    if c == 2:
        cell = z
    elif c == 0:
        cell = x
    else:
        cell = 2 * tile + (iota((1, width), 1) >= half).astype(jnp.int32)
    cell = jnp.asarray(cell, jnp.int32)
    return (row + cell.astype(jnp.float32)) * (SIDES[c] * SCALE)


def halo_kernel(
    sizes, rx, nt, half, count_ref, pos_ref, ext_ref, cen_ref, slot_ref, bound_ref, own, send, recv,
    cen, done,
):
    barrier, arrivals = enter(sizes)
    width = 2 * half
    home = layer_slots(sizes[0])[1][DEPTH]
    wide = iota((1, width), 1)
    for x in range(rx):
        for t in range(nt):
            occupied = occupied_lanes(count_ref, x, t, half)
            for c in range(3):
                rows = [pos_ref[c, 0, x, 2 * t + k : 2 * t + k + 1, :] for k in (0, 1)]
                row = jnp.where(occupied, jnp.concatenate(rows, axis=1), FAR)
                own[x, t, c] = row
                ext_ref[home, x + 1, t + 1, c] = row
    pl.semaphore_wait(barrier, arrivals)

    sub = iota((width, width), 0)
    lane = iota((width, width), 1)
    eye = sub == lane
    same = sub // half == lane // half
    before = sub < lane
    base = jnp.where(wide >= half, half, 0)
    weight = jnp.where(wide >= half, 256.0, 1.0)

    def step(i, carry):
        x, t = i // nt, i % nt
        rows = [own[x, t, c] for c in range(3)]
        bound_ref[0, x, t] = jnp.sum(jnp.where(rows[0] < EDGE, weight, 0.0)).astype(jnp.int32)
        bound_ref[1, x, t] = jnp.sum(jnp.where(rows[0] < 1.0 - EDGE, weight, 0.0)).astype(
            jnp.int32
        )
        key = jnp.broadcast_to(rows[0], (width, width))
        column = jnp.sum(jnp.where(eye, key, 0.0), axis=1, keepdims=True)
        ahead = same & ((column < key) | ((column == key) & before))
        rank = jnp.sum(ahead.astype(jnp.float32), axis=0, keepdims=True)
        slot = rank.astype(jnp.int32) + base
        slot_ref[x, t] = slot
        pick = sub == slot
        for c in range(3):
            row = coordinates(rows[c], c, 0, x, t, half)
            column = jnp.sum(jnp.where(pick, row, 0.0), axis=1, keepdims=True)
            cen[x, t, c] = jnp.broadcast_to(column, (width, width))
        return carry

    split = rx * nt // 2
    stored = pltpu.make_async_copy(cen, cen_ref, done)

    def early():
        lax.fori_loop(0, split, step, 0, unroll=2)

    def late():
        lax.fori_loop(split, rx * nt, step, 0, unroll=2)
        stored.start()

    exchange(sizes, rx, nt, own, ext_ref, send, recv, (early, late))
    stored.wait()


def slope_kernel(sizes, rx, nt, own_ref, ext_ref, send, recv):
    barrier, arrivals = enter(sizes)
    home = layer_slots(sizes[0])[1][DEPTH]
    for x in range(rx):
        for t in range(nt):
            ext_ref[home, x + 1, t + 1, 0] = own_ref[x, t, 0]
    pl.semaphore_wait(barrier, arrivals)
    exchange(sizes, rx, nt, own_ref, ext_ref, send, recv)


def replicate(slots, rx, nt, half, ext_ref, rep_ref, channels, first, absolute):
    width = 2 * half
    low = iota((1, width), 1) < half

    def step(i, carry):
        x, t = i // nt, i % nt
        for z in range(LAYERS):
            for c in range(channels):
                rows = []
                for u in (0, 1, 2):
                    row = ext_ref[slots[z], x, t + u, c]
                    if absolute:
                        row = coordinates(row, c, z - DEPTH, x - 1, t + u - 1, half)
                    rows.append(row)
                mixed = jnp.where(low, rows[2], rows[0])
                rep_ref[x, t, z, first + c] = jnp.broadcast_to(rows[1], (8, width))
                rep_ref[x, t, z, channels_total(rep_ref) // 2 + first + c] = (
                    jnp.broadcast_to(mixed, (8, width))
                )
        return carry

    lax.fori_loop(0, (rx + 2) * nt, step, 0)


def channels_total(rep_ref):
    return rep_ref.shape[3]


def separation(centre, partner):
    deltas = [p - q for p, q in zip(centre, partner)]
    t = REACH - deltas[0] * deltas[0]
    t = t - deltas[1] * deltas[1]
    t = t - deltas[2] * deltas[2]
    return deltas, jnp.maximum(t, 0.0)


def bounds(count_ref, bound_ref, x, t, start, rows):
    lefts, rights = bound_ref[0, x, t], bound_ref[1, x, t]
    left = jnp.maximum(lefts & 255, lefts >> 8)
    first = jnp.where(start < left, 0, 1)
    right = False
    for k, inner in enumerate((rights & 255, rights >> 8)):
        right |= (start + rows > inner) & (start < count_ref[0, x, 2 * t + k])
    return first, jnp.where(right & (first == 0), 3, first + 2)


def groups_of(count_ref, x, t, rows):
    most = jnp.maximum(count_ref[0, x, 2 * t], count_ref[0, x, 2 * t + 1])
    return (most + (rows - 1)) // rows


def occupied_lanes(count_ref, x, t, half):
    lane = iota((1, 2 * half), 1)
    n0, n1 = count_ref[0, x, 2 * t], count_ref[0, x, 2 * t + 1]
    return jnp.where(lane < half, lane - n0, lane - half - n1) < 0


def centres(ref, index, start, rows, half):
    low = iota((rows, 2 * half), 1) < half
    c0 = ref[index + (pl.ds(start, rows),)]
    c1 = ref[index + (pl.ds(half + start, rows),)]
    return c0, c1, jnp.where(low, c1, c0)


def combined(acc, half):
    low = iota(acc[2].shape, 1) < half
    zero = jnp.zeros_like(acc[2])
    return (
        acc[0] + jnp.where(low, zero, acc[2]),
        acc[1] + jnp.where(low, acc[2], zero),
    )


def over(partner, rows):
    return partner if rows == 8 else jnp.concatenate([partner] * (rows // 8), axis=0)


def columns(one, first, last, acc):
    acc = one(first + 1, one(first, acc))
    return lax.fori_loop(first + 2, last, one, acc)


def density_kernel(
    slots, rx, nt, half, rows, count_ref, bound_ref, ext_ref, cen_hbm, slot_ref,
    slope_ref, root_ref, cs_hbm, rep, cen_ref, cs_ref, fetched, stored,
):
    width = 2 * half
    fetch = pltpu.make_async_copy(cen_hbm, cen_ref, fetched)
    fetch.start()
    replicate(slots, rx, nt, half, ext_ref, rep, 3, 0, True)
    fetch.wait()
    sub = iota((width, width), 0)

    def tile(i, carry):
        x, t = i // nt, i % nt

        def group(g, carry):
            start = pl.multiple_of(g * rows, rows)
            cs = [centres(cen_ref, (x, t, c), start, rows, half) for c in range(3)]
            first, last = bounds(count_ref, bound_ref, x, t, start, rows)

            def column(dx, acc):
                acc = list(acc)
                for z in range(LAYERS):
                    for k in range(3):
                        partner = [
                            over(rep[x + dx, t, z, (3 if k == 2 else 0) + c], rows)
                            for c in range(3)
                        ]
                        _, v = separation([c[k] for c in cs], partner)
                        acc[k] = acc[k] + jnp.exp2(v) * (v * v)
                return tuple(acc)

            zero = jnp.zeros((rows, width), jnp.float32)
            acc = columns(column, first, last, (zero,) * 3)
            for k, part in enumerate(combined(acc, half)):
                cs_ref[x, t, pl.ds(k * half + start, rows)] = part
            return carry

        lax.fori_loop(0, groups_of(count_ref, x, t, rows), group, 0)
        total = jnp.sum(cs_ref[x, t], axis=1, keepdims=True) * G1
        pick = sub == slot_ref[x, t]
        one_rho = jnp.sum(jnp.where(pick, total, 0.0), axis=0, keepdims=True)
        occupied = occupied_lanes(count_ref, x, t, half)
        root = jnp.sqrt(jnp.where(occupied, one_rho, 1.0))
        root_ref[x, t] = root
        slope_ref[x, t, 0] = (-0.5 * SIGMA) / root
        cs_ref[x, t] = jnp.broadcast_to((-0.5 * SIGMA) * lax.rsqrt(total), (width, width))
        pltpu.make_async_copy(cs_ref.at[x, t], cs_hbm.at[x, t], stored.at[i]).start()
        return carry

    lax.fori_loop(0, rx * nt, tile, 0)
    for i in range(rx * nt):
        x, t = i // nt, i % nt
        pltpu.make_async_copy(cs_ref.at[x, t], cs_hbm.at[x, t], stored.at[i]).wait()


SIGMA = (3.0 / 16.0) * G1 / G2


def force_kernel(
    slots, rx, nt, half, rows, count_ref, bound_ref, ext_ref, sext_ref, cen_hbm, cs_hbm,
    slot_ref, root_ref, force_ref, energy_ref, rep, out, cen_ref, cs_ref, fetched,
):
    width = 2 * half
    fetches = [
        pltpu.make_async_copy(cen_hbm, cen_ref, fetched.at[0]),
        pltpu.make_async_copy(cs_hbm, cs_ref, fetched.at[1]),
    ]
    for fetch in fetches:
        fetch.start()
    replicate(slots, rx, nt, half, ext_ref, rep, 3, 0, True)
    replicate(slots, rx, nt, half, sext_ref, rep, 1, 3, False)
    for fetch in fetches:
        fetch.wait()
    sub = iota((width, width), 0)

    for x in range(rx):
        for t in range(nt):
            force_tile(
                slots, half, rows, x, t, count_ref, bound_ref, cen_ref, cs_ref, slot_ref,
                root_ref, force_ref, energy_ref, rep, out, sub,
            )


def force_tile(
    slots, half, rows, x, t, count_ref, bound_ref, cen_ref, cs_ref, slot_ref, root_ref,
    force_ref, energy_ref, rep, out, sub,
):
    width = 2 * half

    def group(g, carry):
        start = pl.multiple_of(g * rows, rows)
        cs = [centres(cen_ref, (x, t, c), start, rows, half) for c in range(3)]
        sp = centres(cs_ref, (x, t), start, rows, half)
        first, last = bounds(count_ref, bound_ref, x, t, start, rows)

        def column(dx, acc):
            acc = [list(a) for a in acc]
            for z in range(LAYERS):
                for k in range(3):
                    partner = [
                        over(rep[x + dx, t, z, (4 if k == 2 else 0) + c], rows)
                        for c in range(4)
                    ]
                    d, v = separation([c[k] for c in cs], partner[:3])
                    e1 = jnp.exp2(v)
                    e2 = jnp.exp2(v * (8.0 / 3.0))
                    w = v * e2
                    factor = (sp[k] + partner[3]) * e1 * (v + A) * v + w * (v + B)
                    for c in range(3):
                        acc[c][k] = acc[c][k] + factor * d[c]
                    acc[3][k] = acc[3][k] + w * v
            return tuple(tuple(a) for a in acc)

        zero = jnp.zeros((rows, width), jnp.float32)
        acc = columns(column, first, last, ((zero,) * 3,) * 4)
        for c in range(4):
            for k, part in enumerate(combined(acc[c], half)):
                out[c, pl.ds(k * half + start, rows)] = part
        return carry

    lax.fori_loop(0, groups_of(count_ref, x, t, rows), group, 0)
    pick = sub == slot_ref[x, t]
    occupied = occupied_lanes(count_ref, x, t, half)
    for c in range(4):
        total = jnp.sum(out[c], axis=1, keepdims=True)
        value = jnp.sum(jnp.where(pick, total, 0.0), axis=0, keepdims=True)
        if c < 3:
            value = value * (4.0 / 3.0 * G2 / SCALE)
        else:
            value = value * G2 - 1.0 - root_ref[x, t]
        value = jnp.where(occupied, value, 0.0)
        for k in (0, 1):
            part = value[:, k * half : (k + 1) * half]
            if c < 3:
                force_ref[c, 0, x, 2 * t + k : 2 * t + k + 1, :] = part
            else:
                energy_ref[0, x, 2 * t + k : 2 * t + k + 1, :] = part


def body(positions, counts):
    rx, ry, half = positions.shape[2:]
    nt, width = ry // 2, 2 * half
    f32 = jnp.float32
    sizes = tuple(lax.axis_size(axis) for axis in AXES)
    kept, slots = layer_slots(sizes[0])
    layers, edges, _ = displacements(sizes)
    dma = pltpu.SemaphoreType.DMA
    sems = [dma((len(layers) + len(edges),))] * 2
    centres_buffer = pltpu.VMEM((rx, nt, 3, width, width), f32)
    slopes_buffer = pltpu.VMEM((rx, nt, width, width), f32)

    def shape(*dims, dtype=f32):
        return jax.ShapeDtypeStruct(dims, dtype)

    ext, cen, slot, bound = pl.pallas_call(
        functools.partial(halo_kernel, sizes, rx, nt, half),
        out_shape=(
            shape(len(kept), rx + 2, nt + 2, 3, 1, width),
            shape(rx, nt, 3, width, width),
            shape(rx, nt, 1, width, dtype=jnp.int32),
            shape(2, rx, nt, dtype=jnp.int32),
        ),
        in_specs=[SMEM, VMEM],
        out_specs=(VMEM, ANY, VMEM, SMEM),
        scratch_shapes=[pltpu.VMEM((rx, nt, 3, 1, width), f32)]
        + sems
        + [centres_buffer, dma(())],
        compiler_params=pltpu.CompilerParams(collective_id=0, has_side_effects=True),
        name="halo",
    )(counts, positions)
    slope, root, cs = pl.pallas_call(
        functools.partial(density_kernel, slots, rx, nt, half, 16),
        out_shape=(
            shape(rx, nt, 1, 1, width),
            shape(rx, nt, 1, width),
            shape(rx, nt, width, width),
        ),
        in_specs=[SMEM, SMEM, VMEM, ANY, VMEM],
        out_specs=(VMEM, VMEM, ANY),
        scratch_shapes=[
            pltpu.VMEM((rx + 2, nt, LAYERS, 6, 8, width), f32),
            centres_buffer,
            slopes_buffer,
            dma(()),
            dma((rx * nt,)),
        ],
        name="density",
    )(counts, bound, ext, cen, slot)
    sext = pl.pallas_call(
        functools.partial(slope_kernel, sizes, rx, nt),
        out_shape=shape(len(kept), rx + 2, nt + 2, 1, 1, width),
        in_specs=[VMEM],
        out_specs=VMEM,
        scratch_shapes=sems,
        compiler_params=pltpu.CompilerParams(collective_id=1, has_side_effects=True),
        name="slopes",
    )(slope)
    return pl.pallas_call(
        functools.partial(force_kernel, slots, rx, nt, half, 8),
        out_shape=(shape(3, 1, rx, ry, half), shape(1, rx, ry, half)),
        in_specs=[SMEM, SMEM, VMEM, VMEM, ANY, ANY, VMEM, VMEM],
        out_specs=(VMEM, VMEM),
        scratch_shapes=[
            pltpu.VMEM((rx + 2, nt, LAYERS, 8, 8, width), f32),
            pltpu.VMEM((4, width, width), f32),
            centres_buffer,
            slopes_buffer,
            dma((2,)),
        ],
        name="force",
    )(counts, bound, ext, sext, cen, cs, slot, root)


def solution(mesh):
    return jax.shard_map(
        body,
        mesh=mesh,
        in_specs=(P(None, "gz", "gx", "gy", None), P("gz", "gx", "gy")),
        out_specs=(P(None, "gz", "gx", "gy", None), P("gz", "gx", "gy", None)),
        check_vma=False,
    )
```
